32 devices in a mesh: comp: 4 (over y, core), gx: 2 (over x), gy: 4 (over z).
Axes of the slice: x: 2, y: 2, z: 4, core: 2. Of those that a mesh axis runs over, the one named last changes fastest.
Arguments:
- state: float32 [32, 32, 128, 128], P('comp', 'gx', 'gy'), may hold values from -4 to 4
- levels: int32 [32, 128], P('gx', 'gy'), may hold values from 0 to 128
- reaction: float32 [3, 8, 8], replicated, may hold values from -2 to 2
Outputs:
- new_state: float32 [32, 32, 128, 128], P('comp', 'gx', 'gy')
The draws below stay inside these ranges and needn't reach their ends.
Inputs may be any that keep to these rules, and one draw needn't show every extreme that they name: `levels`: 0 marks a land column, 128 a column of full depth.
All inputs are finite; a program needn't handle non-finite values.
Results may differ from the reference program's by a relative error of at most 0.00018.
Values sent between devices are 32-bit elements; how exact they have to be, the bound alone decides.
No kernel may reach another device: no remote copies, remote signals or barrier semaphores. Data moves between devices by JAX's collectives and lax.ppermute only.
A program may use at most 64 MiB of HBM per device.

```python
import jax
import jax.numpy as jnp
from jax import lax

NF = 8
NZ = 128
ITERS = 3
NFIELDS = 32
NX = 32
NY = 128
N_COMP = 4


def plant(entries, stream_key, low, largest):
    index_at = [jax.random.randint(jax.random.fold_in(stream_key, axis), (), 0, length) for axis, length in enumerate(entries.shape)]
    main_axis = entries.shape.index(max(entries.shape))
    next_to = index_at[:main_axis] + [(index_at[main_axis] + 1) % entries.shape[main_axis]] + index_at[main_axis + 1:]
    return entries.at[tuple(index_at)].set(low).at[tuple(next_to)].set(largest)


def block_levels(stream_key, extent, cuts, least, high):
    loudness, own = 1.0, jax.random.fold_in(stream_key, 6)
    for position, shards_of in cuts:
        steps = jnp.exp(jax.random.uniform(jax.random.fold_in(own, position), (shards_of,), jnp.float32, least / len(cuts), high / len(cuts)))
        loudness = loudness * jnp.repeat(steps, extent[position] // shards_of).reshape([-1 if axis == position else 1 for axis in range(len(extent))])
    return loudness


def noise(key, shape, spread, most, cuts=(), held_as=jnp.bfloat16):
    drawn = jax.random.normal(key, shape, jnp.float32) * spread
    if len(cuts) > 0:
        drawn = block_levels(key, shape, cuts, -0.22, 0.18) * drawn
    return jnp.clip(drawn, min=-most, max=most).astype(held_as)


def setup_inputs(seed: int = 0) -> dict:
    seeds = jax.random.split(jax.random.key(seed), 4)
    state = noise(seeds[0], (NFIELDS, NX, NY, NZ), 0.7, 4.0, ((0, 4), (1, 2), (2, 4)), jnp.float32)
    levels = plant(jax.random.randint(seeds[1], (NX, NY), 0, NZ + 1), jax.random.fold_in(seeds[1], 1), 0, NZ).astype(jnp.int32)
    reaction = noise(seeds[2], (N_COMP - 1, NF, NF), NF ** -0.5, 2.0, (), jnp.float32)
    return dict(state=state, levels=levels, reaction=reaction)


time_step = 0.25
lateral_mix = 0.05
vertical_mix = 0.1
pressure_scale = 0.05
thermal_coef = 1.0
haline_coef = 0.8
coriolis_mean = 0.5
coriolis_slope = 0.5


def along(padded, axis, shift):
    count_x = padded.shape[1] - 4
    count_y = padded.shape[2] - 4
    if axis == 1:
        return padded[:, 2 + shift:2 + shift + count_x, 2:2 + count_y]
    return padded[:, 2:2 + count_x, 2 + shift:2 + shift + count_y]


def centered(padded, axis):
    return (8.0 * (along(padded, axis, 1) - along(padded, axis, -1)) - (along(padded, axis, 2) - along(padded, axis, -2))) / 12.0


def smoothing(padded, axis):
    return (along(padded, axis, 2) + along(padded, axis, -2) - 4.0 * (along(padded, axis, 1) + along(padded, axis, -1)) + 6.0 * along(padded, axis, 0)) / 12.0


def transport(padded, east, north):
    return east * centered(padded, 1) + jnp.abs(east) * smoothing(padded, 1) + north * centered(padded, 2) + jnp.abs(north) * smoothing(padded, 2)


def lateral(padded):
    return along(padded, 1, 1) + along(padded, 1, -1) + along(padded, 2, 1) + along(padded, 2, -1) - 4.0 * along(padded, 1, 0)


def vertical(center):
    column = jnp.pad(center, ((0, 0), (0, 0), (0, 0), (1, 1)))
    return column[..., 2:] + column[..., :-2] - 2.0 * center


def dynamics_step(padded, mask, latitude, accumulate):
    center = padded[:, 2:-2, 2:-2]
    east = center[0]
    north = center[1]
    moving = padded[0:4]
    density = haline_coef * padded[3] - thermal_coef * padded[2]
    pressure = (pressure_scale * accumulate(density))[None]
    tendency = lateral_mix * lateral(moving) + vertical_mix * vertical(center[0:4]) - transport(moving, east, north)
    rotation = (coriolis_mean + coriolis_slope * latitude)[None, :, None]
    push_east = tendency[0] + rotation * north - centered(pressure, 1)[0]
    push_north = tendency[1] - rotation * east - centered(pressure, 2)[0]
    tendency = jnp.stack([push_east, push_north, tendency[2], tendency[3]])
    advanced = center[0:4] + time_step * (1.5 * tendency - 0.5 * center[4:8])
    return jnp.concatenate([advanced * mask, tendency * mask])


def tracer_step(padded, velocity, mask, coupling):
    center = padded[:, 2:-2, 2:-2]
    growth = 2.0 * jax.nn.sigmoid(velocity[2])
    reacting = growth * jnp.einsum("ij,jxyz->ixyz", coupling, center, precision=lax.Precision.HIGHEST)
    tendency = lateral_mix * lateral(padded) + vertical_mix * vertical(center) + reacting - transport(padded, velocity[0], velocity[1])
    return (center + time_step * tendency) * mask


def running_sum(density):
    return jnp.cumsum(density, axis=-1)


def pad_group(group):
    wrapped = jnp.pad(group, ((0, 0), (2, 2), (0, 0), (0, 0)), mode="wrap")
    return jnp.pad(wrapped, ((0, 0), (0, 0), (2, 2), (0, 0)))


def reference(state, levels, reaction):
    depth = jnp.arange(NZ).astype(jnp.int32)
    mask = (depth[None, None, :] < levels[:, :, None]).astype(jnp.float32)
    latitude = 2.0 * jnp.arange(NY).astype(jnp.float32) / (NY - 1) - 1.0
    for step in range(ITERS):
        state = state * mask[None]
        velocity = state[0:3]
        pieces = [dynamics_step(pad_group(state[0:NF]), mask, latitude, running_sum)]
        for group in range(N_COMP - 1):
            block = state[NF * (group + 1):NF * (group + 2)]
            pieces.append(tracer_step(pad_group(block), velocity, mask, reaction[group]))
        state = jnp.concatenate(pieces)
    return state
```

```python
import functools

import jax
import jax.numpy as jnp
from jax import lax
from jax.experimental import pallas as pl
from jax.experimental.pallas import tpu as pltpu
from jax.sharding import PartitionSpec as P

ITERS = 3

time_step = 0.25
lateral_mix = 0.05
vertical_mix = 0.1
pressure_scale = 0.05
thermal_coef = 1.0
haline_coef = 0.8
coriolis_mean = 0.5
coriolis_slope = 0.5

TOP = 8


def padded_copy(pad, q, recv_x, recv_a, recv_b, gy, fields):
    nx, ny = q.shape[1], q.shape[2]
    even = lax.rem(gy, 2) == 0

    @pl.loop(0, fields)
    def _(f):
        for side, first in ((0, 0), (1, nx + 2)):
            for c in range(2):
                pad[f, first + c, TOP : TOP + ny, :] = recv_x[side, f, c]

        @pl.loop(0, nx)
        def _(x):
            pad[f, x + 2, TOP : TOP + ny, :] = q[f, x]

    def rows(high, low):
        @pl.loop(0, fields)
        def _(f):
            for x in range(nx):
                pad[f, x + 2, TOP + ny : TOP + ny + 2, :] = high[f, x]
                pad[f, x + 2, TOP - 2 : TOP, :] = low[f, x]

    @pl.when(even)
    def _():
        rows(recv_a, recv_b)

    @pl.when(jnp.logical_not(even))
    def _():
        rows(recv_b, recv_a)


def send_edges(q, send_x, send_a, send_b, gy, fields):
    nx, ny = q.shape[1], q.shape[2]
    even = lax.rem(gy, 2) == 0

    @pl.loop(0, fields)
    def _(f):
        for side, first in ((0, nx - 2), (1, 0)):
            for c in range(2):
                send_x[side, f, c] = q[f, first + c]

    def rows(high, low):
        @pl.loop(0, fields)
        def _(f):
            for x in range(nx):
                high[f, x] = q[f, x, ny - 2 : ny, :]
                low[f, x] = q[f, x, 0:2, :]

    @pl.when(even)
    def _():
        rows(send_a, send_b)

    @pl.when(jnp.logical_not(even))
    def _():
        rows(send_b, send_a)


def stencil_weights(east, north, scale):
    out = []
    for a in (east, north):
        size = jnp.abs(a)
        mix = scale * lateral_mix
        eight = (scale * 8.0 / 12.0) * a
        four = mix + (scale * 4.0 / 12.0) * size
        one = (scale / 12.0) * a
        low = (-scale / 12.0) * size
        out += [low - one, four + eight, four - eight, low + one]
    center = (-4.0 * scale * lateral_mix) - (scale * 0.5) * (jnp.abs(east) + jnp.abs(north))
    return out, center


def neighbours(pad, f, x, r0, rows):
    return [
        pad[f, x, pl.ds(TOP + r0, rows), :],
        pad[f, x + 1, pl.ds(TOP + r0, rows), :],
        pad[f, x + 3, pl.ds(TOP + r0, rows), :],
        pad[f, x + 4, pl.ds(TOP + r0, rows), :],
        pad[f, x + 2, pl.ds(TOP + r0 - 2, rows), :],
        pad[f, x + 2, pl.ds(TOP + r0 - 1, rows), :],
        pad[f, x + 2, pl.ds(TOP + r0 + 1, rows), :],
        pad[f, x + 2, pl.ds(TOP + r0 + 2, rows), :],
    ]


def weighted(weights, values):
    total = None
    for w, v in zip(weights, values):
        term = w * v
        total = term if total is None else total + term
    return total


def vertical_weights(rows, depth, scale):
    k = lax.broadcasted_iota(jnp.int32, (rows, depth), 1)
    zero = jnp.zeros((rows, depth), jnp.float32)
    above = jnp.where(k == 0, zero, scale)
    below = jnp.where(k == depth - 1, zero, scale)
    return above, below


def tracer_update(pad, mask, vel, coupling, new, rows):
    nx, ny, depth = mask.shape
    scale = time_step
    above, below = vertical_weights(rows, depth, scale * vertical_mix)
    fields = new.shape[0]
    for r0 in range(0, ny, rows):

        @pl.loop(0, nx)
        def _(x):
            here = [pad[f, x + 2, pl.ds(TOP + r0, rows), :] for f in range(fields)]
            for i in range(fields):
                total = coupling[i, 0] * here[0]
                for j in range(1, fields):
                    total = total + coupling[i, j] * here[j]
                new[i, x, pl.ds(r0, rows), :] = total

        @pl.loop(0, nx)
        def _(x):
            east = vel[0, x, pl.ds(r0, rows), :]
            north = vel[1, x, pl.ds(r0, rows), :]
            growth = (2.0 * scale) * jax.nn.sigmoid(vel[2, x, pl.ds(r0, rows), :])
            sea = mask[x, pl.ds(r0, rows), :]
            weights, center = stencil_weights(east, north, scale)
            center = center + (1.0 - 2.0 * scale * vertical_mix)
            for f in range(fields):
                q = pad[f, x + 2, pl.ds(TOP + r0, rows), :]
                total = weighted(weights, neighbours(pad, f, x, r0, rows))
                total = total + center * q
                total = total + above * pltpu.roll(q, 1, 1)
                total = total + below * pltpu.roll(q, depth - 1, 1)
                total = total + growth * new[f, x, pl.ds(r0, rows), :]
                new[f, x, pl.ds(r0, rows), :] = sea * total


def dynamics_update(pad, q, mask, slope, new, gy, total_rows, rows):
    nx, ny, depth = mask.shape
    rho = 4

    @pl.loop(0, nx + 4)
    def _(x):
        pad[rho, x] = haline_coef * pad[3, x] - thermal_coef * pad[2, x]

    @pl.loop(0, nx)
    def _(x):
        n = neighbours(pad, rho, x, 0, ny)
        first = pressure_scale * 8.0 / 12.0
        second = pressure_scale / 12.0
        slope[0, x] = first * (n[2] - n[1]) - second * (n[3] - n[0])
        slope[1, x] = first * (n[6] - n[5]) - second * (n[7] - n[4])

    lower = lax.broadcasted_iota(jnp.int32, (depth, depth), 0)
    higher = lax.broadcasted_iota(jnp.int32, (depth, depth), 1)
    summing = (lower <= higher).astype(jnp.float32)
    for axis in range(2):

        @pl.loop(0, nx, step=4)
        def _(x):
            part = slope[axis, pl.ds(x, 4)].reshape(4 * ny, depth)
            summed = jnp.dot(
                part,
                summing,
                precision=lax.Precision.HIGHEST,
                preferred_element_type=jnp.float32,
            )
            slope[axis, pl.ds(x, 4)] = summed.reshape(4, ny, depth)

    above, below = vertical_weights(rows, depth, vertical_mix)
    for r0 in range(0, ny, rows):
        row = gy * ny + r0 + lax.broadcasted_iota(jnp.int32, (rows, depth), 0)
        latitude = row.astype(jnp.float32) * (2.0 / float(total_rows - 1)) - 1.0
        rotation = coriolis_mean + coriolis_slope * latitude

        @pl.loop(0, nx)
        def _(x):
            here = [pad[f, x + 2, pl.ds(TOP + r0, rows), :] for f in range(4)]
            sea = mask[x, pl.ds(r0, rows), :]
            weights, center = stencil_weights(here[0], here[1], 1.0)
            center = center - 2.0 * vertical_mix
            for f in range(4):
                total = weighted(weights, neighbours(pad, f, x, r0, rows))
                total = total + center * here[f]
                total = total + above * pltpu.roll(here[f], 1, 1)
                total = total + below * pltpu.roll(here[f], depth - 1, 1)
                if f == 0:
                    total = total + rotation * here[1] - slope[0, x, pl.ds(r0, rows), :]
                if f == 1:
                    total = total - rotation * here[0] - slope[1, x, pl.ds(r0, rows), :]
                previous = q[4 + f, x, pl.ds(r0, rows), :]
                moved = here[f] + (1.5 * time_step) * total - (0.5 * time_step) * previous
                new[f, x, pl.ds(r0, rows), :] = sea * moved
                new[4 + f, x, pl.ds(r0, rows), :] = sea * total


def step_kernel(last, total_rows, q, mask, recv_x, recv_a, recv_b, kept, came, coupling, *rest):
    if last:
        new, pad, slope, vel = rest
    else:
        new, send_x, send_a, send_b, speed, pad, slope, vel = rest
    slot = lax.axis_index("comp")
    gy = lax.axis_index("gy")
    fields = q.shape[0]

    @pl.when(slot == 0)
    def _():
        padded_copy(pad, q, recv_x, recv_a, recv_b, gy, 4)
        dynamics_update(pad, q, mask, slope, new, gy, total_rows, 16)
        if not last:
            speed[...] = new[0:3]

    @pl.when(slot > 0)
    def _():
        padded_copy(pad, q, recv_x, recv_a, recv_b, gy, fields)

        @pl.when(lax.rem(slot, 2) == 0)
        def _():
            vel[...] = kept[...]

        @pl.when(lax.rem(slot, 2) == 1)
        def _():
            vel[...] = came[...]

        tracer_update(pad, mask, vel, coupling, new, 16)

    if not last:
        send_edges(new, send_x, send_a, send_b, gy, fields)


def start_kernel(state, mask, q, send_x, send_a, send_b, speed):
    gy = lax.axis_index("gy")
    fields, nx = state.shape[:2]

    @pl.loop(0, fields)
    def _(f):
        @pl.loop(0, nx)
        def _(x):
            q[f, x] = state[f, x] * mask[x]

    speed[...] = q[0:3]
    send_edges(q, send_x, send_a, send_b, gy, fields)


def vmem_specs(count):
    return [pl.BlockSpec(memory_space=pltpu.VMEM)] * count


PARAMS = pltpu.CompilerParams(vmem_limit_bytes=24 * 1024 * 1024)


def per_device(state, levels, reaction):
    fields, nx, ny, depth = state.shape
    comp_count = lax.axis_size("comp")
    gx_count = lax.axis_size("gx")
    gy_count = lax.axis_size("gy")
    slot = lax.axis_index("comp")
    total_rows = ny * gy_count
    level = lax.broadcasted_iota(jnp.int32, (1, 1, depth), 2)
    mask = (level < levels[:, :, None]).astype(jnp.float32)
    coupling = lax.dynamic_index_in_dim(reaction, jnp.maximum(slot - 1, 0), 0, keepdims=False)

    f32 = functools.partial(jax.ShapeDtypeStruct, dtype=jnp.float32)
    whole = f32((fields, nx, ny, depth))
    sends = [
        f32((2, fields, 2, ny, depth)),
        f32((fields, nx, 2, depth)),
        f32((fields, nx, 2, depth)),
        f32((3, nx, ny, depth)),
    ]

    def exchange_x(send):
        if gx_count == 2:
            return lax.ppermute(send, "gx", [(0, 1), (1, 0)])
        tail = lax.ppermute(send[0], "gx", [(i, (i + 1) % gx_count) for i in range(gx_count)])
        head = lax.ppermute(send[1], "gx", [((i + 1) % gx_count, i) for i in range(gx_count)])
        return jnp.stack([tail, head])

    def exchange_y(send, first):
        pairs = []
        for i in range(first, gy_count - 1, 2):
            pairs += [(i, i + 1), (i + 1, i)]
        return lax.ppermute(send, "gy", pairs)

    def spread(speed):
        hop = 1
        while hop * 2 < comp_count:
            hop *= 2
        kept, came = speed, speed
        while hop >= 1:
            came = lax.ppermute(
                kept, "comp", [(i, i + hop) for i in range(0, comp_count - hop, 2 * hop)]
            )
            if hop > 1:
                kept = jnp.where(lax.rem(slot, 2 * hop) == 0, kept, came)
            hop //= 2
        return kept, came

    q, send_x, send_a, send_b, speed = pl.pallas_call(
        start_kernel,
        out_shape=[whole] + sends,
        in_specs=vmem_specs(2),
        out_specs=vmem_specs(5),
        compiler_params=PARAMS,
        name="start",
    )(state, mask)
    for step in range(ITERS):
        last = step == ITERS - 1
        kept, came = spread(speed)
        recv_x = exchange_x(send_x)
        recv_a = exchange_y(send_a, 0)
        recv_b = exchange_y(send_b, 1)
        out = pl.pallas_call(
            functools.partial(step_kernel, last, total_rows),
            out_shape=[whole] if last else [whole] + sends,
            in_specs=vmem_specs(7) + [pl.BlockSpec(memory_space=pltpu.SMEM)],
            out_specs=vmem_specs(1 if last else 5),
            scratch_shapes=[
                pltpu.VMEM((fields, nx + 4, ny + 16, depth), jnp.float32),
                pltpu.VMEM((2, nx, ny, depth), jnp.float32),
                pltpu.VMEM((3, nx, ny, depth), jnp.float32),
            ],
            compiler_params=PARAMS,
            name="step",
        )(q, mask, recv_x, recv_a, recv_b, kept, came, coupling)
        if last:
            (q,) = out
        else:
            q, send_x, send_a, send_b, speed = out
    return q


def solution(mesh):
    in_specs = (P("comp", "gx", "gy", None), P("gx", "gy"), P())
    out_specs = P("comp", "gx", "gy", None)
    return jax.shard_map(
        per_device, mesh=mesh, in_specs=in_specs, out_specs=out_specs, check_vma=False
    )
```
